32 devices in a mesh: group: 2 (over x), wide: 16 (over z, y, core).
Axes of the slice: x: 2, y: 2, z: 4, core: 2. Of those that a mesh axis runs over, the one named last changes fastest.
Arguments:
- block_input: bfloat16 [32, 512, 1024], P(('group', 'wide')), may hold values from -6 to 6
- out_cotangent: bfloat16 [32, 512, 1024], P(('group', 'wide')), may hold values from -6 to 6
- segment_ids: int32 [32, 512], P(('group', 'wide')), may hold values from 0 to 13, as said below
- document_start: int32 [32, 512], P(('group', 'wide')), may hold values from 0 to 16383, as said below
- mixer_master: float32 [4196352], P(('group', 'wide'))
- feed_master: float32 [8060928], P(('group', 'wide'))
- mixer_first: float32 [4196352], P(('group', 'wide'))
- feed_first: float32 [8060928], P(('group', 'wide'))
- mixer_second: float32 [4196352], P(('group', 'wide'))
- feed_second: float32 [8060928], P(('group', 'wide'))
Outputs:
- block_output: bfloat16 [32, 512, 1024], P(('group', 'wide'))
- input_gradient: float32 [32, 512, 1024], P(('group', 'wide'))
- mixer_gradient: float32 [4196352], P(('group', 'wide'))
- feed_gradient: float32 [8060928], P(('group', 'wide'))
- mixer_new: float32 [4196352], P(('group', 'wide'))
- feed_new: float32 [8060928], P(('group', 'wide'))
- mixer_first_new: float32 [4196352], P(('group', 'wide'))
- feed_first_new: float32 [8060928], P(('group', 'wide'))
- mixer_second_new: float32 [4196352], P(('group', 'wide'))
- feed_second_new: float32 [8060928], P(('group', 'wide'))
The draws below stay inside these ranges and needn't reach their ends.
Inputs may be any that keep to these rules, and one draw needn't show every extreme that they name: `segment_ids`: along the flattened order of sequences and tokens the numbers never fall and rise by one at the first token of each document; a document has 204 to 2048 tokens, except the last one, which the end of the stream may cut; the first document has exactly 2048. `document_start`: equal for all tokens of one document and equal to the flattened index of that document's first token.
All inputs are finite; a program needn't handle non-finite values.
Results may differ from the reference program's by a relative error of at most 0.03.
The reference program's roundings to bfloat16 on the way count: a program that leaves them out, or rounds other values in their place, can miss the bound.
Values may be sent and summed in bfloat16 or wider, within the bound.
No kernel may reach another device: no remote copies, remote signals or barrier semaphores. Data moves between devices by JAX's collectives and lax.ppermute only.
A program may use at most 256 MiB of HBM per device.

```python
import jax
import jax.numpy as jnp
from jax import lax

D = 1024
HEADS = 16
HEAD_DIM = 64
FF = 2624
SEQ_LEN = 512
SEQS = 32
DOC_MIN = 204
DOC_MAX = 2048
PA = 4196352
PF = 8060928


def documents(key):
    count_all = SEQS * SEQ_LEN
    middle_length = (DOC_MIN + DOC_MAX) // 2
    pair_total = 2 * middle_length
    rest_tokens = count_all - DOC_MAX
    pair_count = rest_tokens // pair_total
    tail_length = rest_tokens % pair_total
    offsets = jax.random.randint(jax.random.fold_in(key, 11), (pair_count,), 0, middle_length - DOC_MIN + 1).astype(jnp.int32)
    paired = jnp.concatenate([middle_length + offsets, middle_length - offsets])
    order = jax.random.permutation(jax.random.fold_in(key, 12), 2 * pair_count)
    paired = paired[order]
    lengths = jnp.concatenate([jnp.full((1,), DOC_MAX, jnp.int32), paired.astype(jnp.int32), jnp.full((1,), tail_length, jnp.int32)])
    finish = jnp.cumsum(lengths).astype(jnp.int32)
    starts = finish - lengths
    flat_index = jnp.arange(count_all, dtype=jnp.int32)
    document = jnp.searchsorted(finish, flat_index, side='right').astype(jnp.int32)
    return (document.reshape(SEQS, SEQ_LEN), starts[document].reshape(SEQS, SEQ_LEN))


def unit_noise(key, entries):
    return jax.random.normal(key, (entries,), jnp.float32)


def draw_block_input(key, part):
    array_shape = (SEQS, SEQ_LEN, D)
    values = jnp.clip(jax.random.normal(jax.random.fold_in(key, 23), array_shape, jnp.float32), -6.0, 6.0)
    return values.astype(jnp.bfloat16)


def draw_segment_ids(key, part):
    return documents(key)[0]


def draw_document_start(key, part):
    return documents(key)[1]


def draw_mixer_master(key, part):
    gains = 1.0 + 0.1 * unit_noise(jax.random.fold_in(key, 1), 2 * D)
    project = (unit_noise(jax.random.fold_in(key, 2), 3 * D * D) * D ** (-0.5)).reshape(D, 3, HEADS, HEAD_DIM)
    project = project.reshape(-1)
    output = unit_noise(jax.random.fold_in(key, 3), D * D) * (6.0 * D ** (-0.5))
    return jnp.concatenate([gains, project, output])


def draw_feed_master(key, part):
    expand = unit_noise(jax.random.fold_in(key, 4), 2 * D * FF) * D ** (-0.5)
    contract = unit_noise(jax.random.fold_in(key, 5), FF * D) * FF ** (-0.5)
    return jnp.concatenate([expand, contract])


def moment_scale():
    return (4 * D * D + 2 * D + 3 * D * FF) ** (-0.5)


def draw_mixer_first(key, part):
    return unit_noise(jax.random.fold_in(key, 6), 4 * D * D + 2 * D) * (0.1 * moment_scale())


def draw_feed_first(key, part):
    return unit_noise(jax.random.fold_in(key, 7), 3 * D * FF) * (0.1 * moment_scale())


def second_draw(key, entries):
    spread = jnp.exp(jax.random.uniform(key, (entries,), jnp.float32, -1.2039728, 1.0986123))
    return spread * (0.001 * moment_scale() * moment_scale())


def draw_mixer_second(key, part):
    return second_draw(jax.random.fold_in(key, 8), 4 * D * D + 2 * D)


def draw_feed_second(key, part):
    return second_draw(jax.random.fold_in(key, 9), 3 * D * FF)


def block_scale(stream_key, extent, cuts, low, largest):
    gain = 1.0
    for axis_at, shards_of in cuts:
        heights = jax.random.uniform(jax.random.fold_in(jax.random.fold_in(stream_key, 6), axis_at), (shards_of,), jnp.float32, low / len(cuts), largest / len(cuts))
        gain = gain * jnp.repeat(jnp.exp(heights), extent[axis_at] // shards_of).reshape((-1,) + (1,) * (len(extent) - 1 - axis_at))
    return gain


def normal_values(key, dims, deviation, reach, shards=(), held_as=jnp.bfloat16):
    gain = block_scale(key, dims, shards, -0.22, 0.18) if shards else 1.0
    values = jax.random.normal(key, dims, jnp.float32) * deviation * gain
    return jnp.minimum(jnp.maximum(values, -reach), reach).astype(held_as)


def setup_inputs(seed: int = 0) -> dict:
    streams_of = jax.random.split(jax.random.key(seed), 11)
    return {
        "block_input": draw_block_input(jax.random.fold_in(streams_of[10], 71), 0),
        "out_cotangent": normal_values(streams_of[1], (SEQS, SEQ_LEN, D), 1.0, 6.0, ((0, 32),)),
        "segment_ids": draw_segment_ids(jax.random.fold_in(streams_of[10], 71), 0),
        "document_start": draw_document_start(jax.random.fold_in(streams_of[10], 71), 0),
        "mixer_master": draw_mixer_master(jax.random.fold_in(streams_of[10], 71), 0),
        "feed_master": draw_feed_master(jax.random.fold_in(streams_of[10], 71), 0),
        "mixer_first": draw_mixer_first(jax.random.fold_in(streams_of[10], 71), 0),
        "feed_first": draw_feed_first(jax.random.fold_in(streams_of[10], 71), 0),
        "mixer_second": draw_mixer_second(jax.random.fold_in(streams_of[10], 71), 0),
        "feed_second": draw_feed_second(jax.random.fold_in(streams_of[10], 71), 0),
    }


norm_epsilon = 1e-05
rope_base = 160000.0
masked_score = -1e+30
beta_one = 0.9
beta_two = 0.999
adam_epsilon = 1e-08
learn_rate = 0.002
decay_rate = 0.01
adam_step = 2.0
clip_norm = 1.0

def widen_float(values):
    return values.astype(jnp.float32)

def layer_norm(values, norm_gain):
    row_mean = lax.optimization_barrier(jnp.mean(values, axis=-1, keepdims=True))
    centred = values - row_mean
    variance = lax.optimization_barrier(jnp.mean(centred * centred, axis=-1, keepdims=True))
    reciprocal = lax.rsqrt(variance + norm_epsilon)
    normed = centred * reciprocal
    return (normed * norm_gain, normed, reciprocal)

def norm_backward(upstream, normed, reciprocal, norm_gain):
    scaled = upstream * norm_gain
    first_mean = lax.optimization_barrier(jnp.mean(scaled, axis=-1, keepdims=True))
    second_mean = lax.optimization_barrier(jnp.mean(scaled * normed, axis=-1, keepdims=True))
    return (reciprocal * (scaled - first_mean - normed * second_mean), lax.optimization_barrier(jnp.sum(upstream * normed, axis=0)))

def rope_tables(positions, head_size):
    half_size = head_size // 2
    exponent = jnp.arange(half_size, dtype=jnp.float32) * (2.0 / head_size)
    inverse = rope_base ** (-exponent)
    angles = positions.astype(jnp.float32)[..., None] * inverse
    return (jnp.cos(angles), jnp.sin(angles))

def rotate_pairs(values, cosine, sine_part):
    half_size = values.shape[-1] // 2
    first_half = values[..., :half_size]
    second_half = values[..., half_size:]
    cosine_rows = cosine[..., None, :]
    sine_rows = sine_part[..., None, :]
    return jnp.concatenate([first_half * cosine_rows - second_half * sine_rows, second_half * cosine_rows + first_half * sine_rows], axis=-1)

def gelu_parts(gelu_input):
    normal_cdf = 0.5 * (1.0 + jax.scipy.special.erf(gelu_input * 0.7071067811865476))
    density = jnp.exp(-0.5 * gelu_input * gelu_input) * 0.3989422804014327
    return (gelu_input * normal_cdf, normal_cdf + gelu_input * density)

def unpack_weights(mixer_flat, feed_flat, width):
    hidden_units = feed_flat.shape[0] // (3 * width)
    gain_first = mixer_flat[:width].astype(jnp.float32)
    gain_second = mixer_flat[width:2 * width].astype(jnp.float32)
    project_end = 2 * width + 3 * width * width
    weight_project = mixer_flat[2 * width:project_end].reshape(width, 3 * width)
    weight_output = mixer_flat[project_end:].reshape(width, width)
    weight_expand = feed_flat[:2 * width * hidden_units].reshape(width, 2 * hidden_units)
    weight_contract = feed_flat[2 * width * hidden_units:].reshape(hidden_units, width)
    return (gain_first, gain_second, weight_project, weight_output, weight_expand, weight_contract)

def optimizer_step(master, first, second, gradient, clip_factor):
    clipped = gradient * clip_factor
    first_new = beta_one * first + (1.0 - beta_one) * clipped
    second_new = beta_two * second + (1.0 - beta_two) * clipped * clipped
    first_fixed = first_new / (1.0 - beta_one ** adam_step)
    second_fixed = second_new / (1.0 - beta_two ** adam_step)
    master_new = master - learn_rate * (first_fixed / (jnp.sqrt(second_fixed) + adam_epsilon) + decay_rate * master)
    return (master_new, first_new, second_new)

def sequence_pass(weights, block_rows, cotangent, segment_row, start_row, first_index):
    gain_first, gain_second, weight_project, weight_output, weight_expand, weight_contract = weights
    sequence_length, width = block_rows.shape
    head_size = width // HEADS
    score_scale = head_size ** (-0.5)
    hidden_units = weight_contract.shape[0]
    positions = first_index + jnp.arange(sequence_length, dtype=jnp.int32) - start_row
    cosine, sine_part = rope_tables(positions, head_size)
    residual_in = block_rows.astype(jnp.float32)
    normed_out, normed_one, spread_one = layer_norm(residual_in, gain_first)
    hidden_one = normed_out.astype(jnp.bfloat16)
    projected = jnp.dot(hidden_one, weight_project, preferred_element_type=jnp.float32).reshape(sequence_length, 3, HEADS, head_size)
    query_rope = rotate_pairs(projected[:, 0], cosine, sine_part).astype(jnp.bfloat16)
    key_rope = rotate_pairs(projected[:, 1], cosine, sine_part).astype(jnp.bfloat16)
    value_rows = projected[:, 2].astype(jnp.bfloat16)
    same_document = (segment_row[:, None] == segment_row[None, :])[None]
    scores = jnp.einsum('qhd,khd->hqk', widen_float(query_rope), widen_float(key_rope)) * score_scale
    scores = jnp.where(same_document, scores, masked_score)
    row_peak = lax.optimization_barrier(jnp.max(scores, axis=-1, keepdims=True))
    log_total = row_peak + jnp.log(lax.optimization_barrier(jnp.sum(jnp.exp(scores - row_peak), axis=-1, keepdims=True)))
    softmax_out = jnp.exp(scores - log_total)
    softmax_low = softmax_out.astype(jnp.bfloat16)
    context_heads = jnp.einsum('hqk,khd->qhd', widen_float(softmax_low), widen_float(value_rows)).astype(jnp.bfloat16)
    context = context_heads.reshape(sequence_length, width)
    residual_mid = residual_in + jnp.dot(context, weight_output, preferred_element_type=jnp.float32)
    normed_out, normed_two, spread_two = layer_norm(residual_mid, gain_second)
    hidden_two = normed_out.astype(jnp.bfloat16)
    expanded = jnp.dot(hidden_two, weight_expand, preferred_element_type=jnp.float32)
    gelu_input = expanded[:, :hidden_units]
    gate_part = expanded[:, hidden_units:]
    activated, gelu_slope = gelu_parts(gelu_input)
    product = (activated * gate_part).astype(jnp.bfloat16)
    block_out = (residual_mid + jnp.dot(product, weight_contract, preferred_element_type=jnp.float32)).astype(jnp.bfloat16)
    upstream = cotangent.astype(jnp.float32)
    back_contract = jnp.dot(product.T, cotangent, preferred_element_type=jnp.float32)
    back_product = jnp.dot(cotangent, weight_contract.T, preferred_element_type=jnp.float32)
    back_expanded = jnp.concatenate([back_product * gate_part * gelu_slope, back_product * activated], axis=1).astype(jnp.bfloat16)
    back_expand = jnp.dot(hidden_two.T, back_expanded, preferred_element_type=jnp.float32)
    back_hidden = jnp.dot(back_expanded, weight_expand.T, preferred_element_type=jnp.float32)
    back_norm, back_gain_two = norm_backward(back_hidden, normed_two, spread_two, gain_second)
    back_mid = upstream + back_norm
    back_mid_low = back_mid.astype(jnp.bfloat16)
    back_output = jnp.dot(context.T, back_mid_low, preferred_element_type=jnp.float32)
    back_context = jnp.dot(back_mid_low, weight_output.T, preferred_element_type=jnp.float32).astype(jnp.bfloat16).reshape(sequence_length, HEADS, head_size)
    row_delta = lax.optimization_barrier(jnp.sum(widen_float(back_context) * widen_float(context_heads), axis=-1)).T[:, :, None]
    back_values = jnp.einsum('hqk,qhd->khd', widen_float(softmax_low), widen_float(back_context))
    back_soft = jnp.einsum('qhd,khd->hqk', widen_float(back_context), widen_float(value_rows))
    back_scores = (softmax_out * (back_soft - row_delta) * score_scale).astype(jnp.bfloat16)
    back_query = jnp.einsum('hqk,khd->qhd', widen_float(back_scores), widen_float(key_rope))
    back_key = jnp.einsum('hqk,qhd->khd', widen_float(back_scores), widen_float(query_rope))
    back_query = rotate_pairs(back_query, cosine, -sine_part)
    back_key = rotate_pairs(back_key, cosine, -sine_part)
    back_projected = jnp.stack([back_query, back_key, back_values], axis=1).reshape(sequence_length, 3 * width).astype(jnp.bfloat16)
    back_project = jnp.dot(hidden_one.T, back_projected, preferred_element_type=jnp.float32)
    back_hidden = jnp.dot(back_projected, weight_project.T, preferred_element_type=jnp.float32)
    back_norm, back_gain_one = norm_backward(back_hidden, normed_one, spread_one, gain_first)
    input_grad = back_mid + back_norm
    mixer_piece = jnp.concatenate([back_gain_one, back_gain_two, back_project.reshape(-1), back_output.reshape(-1)])
    feed_piece = jnp.concatenate([back_expand.reshape(-1), back_contract.reshape(-1)])
    return (block_out, input_grad, mixer_piece, feed_piece)

def reference(block_input, out_cotangent, segment_ids, document_start, mixer_master, feed_master, mixer_first, feed_first, mixer_second, feed_second):
    weights = unpack_weights(mixer_master.astype(jnp.bfloat16), feed_master.astype(jnp.bfloat16), D)
    first_index = jnp.arange(SEQS, dtype=jnp.int32) * SEQ_LEN

    def visit_sequence(running, seq_item):
        block_rows, cotangent, segment_row, start_row, first_row = seq_item
        block_out, input_grad, mixer_piece, feed_piece = sequence_pass(weights, block_rows, cotangent, segment_row, start_row, first_row)
        return ((running[0] + mixer_piece, running[1] + feed_piece), (block_out, input_grad))
    zero_grads = (jnp.zeros((PA,), jnp.float32), jnp.zeros((PF,), jnp.float32))
    sums, outputs = lax.scan(visit_sequence, zero_grads, (block_input, out_cotangent, segment_ids, document_start, first_index))
    mixer_gradient, feed_gradient = sums
    block_output, input_gradient = outputs
    square_total = jnp.sum(mixer_gradient * mixer_gradient) + jnp.sum(feed_gradient * feed_gradient)
    clip_factor = jnp.minimum(1.0, clip_norm / (jnp.sqrt(square_total) + 1e-06))
    mixer_new, mixer_first_new, mixer_second_new = optimizer_step(mixer_master, mixer_first, mixer_second, mixer_gradient, clip_factor)
    feed_new, feed_first_new, feed_second_new = optimizer_step(feed_master, feed_first, feed_second, feed_gradient, clip_factor)
    return (block_output, input_gradient, mixer_gradient, feed_gradient, mixer_new, feed_new, mixer_first_new, feed_first_new, mixer_second_new, feed_second_new)
```

```python
import functools

import jax
import jax.numpy as jnp
from jax import lax
from jax.sharding import PartitionSpec as P

HEADS = 16


norm_epsilon = 1e-05
rope_base = 160000.0
masked_score = -1e30
beta_one = 0.9
beta_two = 0.999
adam_epsilon = 1e-08
learn_rate = 0.002
decay_rate = 0.01
adam_step = 2.0
clip_norm = 1.0


def layer_norm(values, norm_gain):
    row_mean = jnp.mean(values, axis=-1, keepdims=True)
    centred = values - row_mean
    variance = jnp.mean(centred * centred, axis=-1, keepdims=True)
    reciprocal = lax.rsqrt(variance + norm_epsilon)
    normed = centred * reciprocal
    return (normed * norm_gain, normed, reciprocal)


def norm_backward(upstream, normed, reciprocal, norm_gain):
    scaled = upstream * norm_gain
    first_mean = jnp.mean(scaled, axis=-1, keepdims=True)
    second_mean = jnp.mean(scaled * normed, axis=-1, keepdims=True)
    return (
        reciprocal * (scaled - first_mean - normed * second_mean),
        jnp.sum(upstream * normed, axis=0),
    )


def rope_tables(positions, head_size):
    half_size = head_size // 2
    exponent = jnp.arange(half_size, dtype=jnp.float32) * (2.0 / head_size)
    inverse = rope_base ** (-exponent)
    angles = positions.astype(jnp.float32)[..., None] * inverse
    return (jnp.cos(angles), jnp.sin(angles))


def rotate_pairs(values, cosine, sine_part):
    half_size = values.shape[-1] // 2
    first_half = values[..., :half_size]
    second_half = values[..., half_size:]
    cosine_rows = cosine[..., None, :]
    sine_rows = sine_part[..., None, :]
    return jnp.concatenate(
        [
            first_half * cosine_rows - second_half * sine_rows,
            second_half * cosine_rows + first_half * sine_rows,
        ],
        axis=-1,
    )


def gelu_parts(gelu_input):
    normal_cdf = 0.5 * (1.0 + jax.scipy.special.erf(gelu_input * 0.7071067811865476))
    density = jnp.exp(-0.5 * gelu_input * gelu_input) * 0.3989422804014327
    return (gelu_input * normal_cdf, normal_cdf + gelu_input * density)


def optimizer_step(master, first, second, gradient, clip_factor):
    clipped = gradient * clip_factor
    first_new = beta_one * first + (1.0 - beta_one) * clipped
    second_new = beta_two * second + (1.0 - beta_two) * clipped * clipped
    first_fixed = first_new / (1.0 - beta_one**adam_step)
    second_fixed = second_new / (1.0 - beta_two**adam_step)
    master_new = master - learn_rate * (
        first_fixed / (jnp.sqrt(second_fixed) + adam_epsilon) + decay_rate * master
    )
    return (master_new, first_new, second_new)


def masked_scores(query_rope, key_rope, segment_row):
    score_scale = query_rope.shape[-1] ** (-0.5)
    scores = (
        jnp.einsum("qhd,khd->hqk", query_rope, key_rope, preferred_element_type=jnp.float32)
        * score_scale
    )
    same_document = (segment_row[:, None] == segment_row[None, :])[None]
    return jnp.where(same_document, scores, masked_score)


def attend_forward(seq_item):
    query_rope, key_rope, value_rows, segment_row = seq_item
    scores = masked_scores(query_rope, key_rope, segment_row)
    row_peak = jnp.max(scores, axis=-1, keepdims=True)
    log_total = row_peak + jnp.log(jnp.sum(jnp.exp(scores - row_peak), axis=-1, keepdims=True))
    softmax_low = jnp.exp(scores - log_total).astype(jnp.bfloat16)
    context = jnp.einsum(
        "hqk,khd->qhd", softmax_low, value_rows, preferred_element_type=jnp.float32
    ).astype(jnp.bfloat16)
    return (context, log_total)


def attend_backward(seq_item):
    query_rope, key_rope, value_rows, segment_row, log_total, back_context, context = seq_item
    score_scale = query_rope.shape[-1] ** (-0.5)
    scores = masked_scores(query_rope, key_rope, segment_row)
    softmax_out = jnp.exp(scores - log_total)
    softmax_low = softmax_out.astype(jnp.bfloat16)
    row_delta = jnp.sum(back_context.astype(jnp.float32) * context.astype(jnp.float32), axis=-1).T[
        :, :, None
    ]
    back_values = jnp.einsum(
        "hqk,qhd->khd", softmax_low, back_context, preferred_element_type=jnp.float32
    )
    back_soft = jnp.einsum(
        "qhd,khd->hqk", back_context, value_rows, preferred_element_type=jnp.float32
    )
    back_scores = (softmax_out * (back_soft - row_delta) * score_scale).astype(jnp.bfloat16)
    back_query = jnp.einsum(
        "hqk,khd->qhd", back_scores, key_rope, preferred_element_type=jnp.float32
    )
    back_key = jnp.einsum(
        "hqk,qhd->khd", back_scores, query_rope, preferred_element_type=jnp.float32
    )
    return (back_query, back_key, back_values)

CORES = 2


def device_layout(mesh_sizes):
    group_size, wide_size = mesh_sizes
    return group_size, wide_size // (2 * CORES), 2


class Wires:
    def __init__(self, group_size, line_size, pair_size):
        self.sizes = (group_size, line_size, pair_size, CORES)
        index = lax.axis_index(("group", "wide"))
        self.core = index % CORES
        self.pair = index // CORES % pair_size
        self.line = index // (CORES * pair_size) % line_size
        self.group = index // (CORES * pair_size * line_size)
        self.index = index
        self.chip = index // CORES

    def send(self, value, group=0, line=0, pair=0, core=0):
        shift = (group, line, pair, core)
        pairs = []
        total = 1
        for size in self.sizes:
            total *= size
        for source in range(total):
            rest, place = source, []
            for size in reversed(self.sizes):
                place.append(rest % size)
                rest //= size
            place = place[::-1]
            target = 0
            for size, at, move in zip(self.sizes, place, shift):
                target = target * size + (at + move) % size
            pairs.append((source, target))
        return lax.ppermute(value, ("group", "wide"), pairs)

    def gather_chips(self, slot):
        group_size, line_size, pair_size, _ = self.sizes
        line_all = jnp.zeros((line_size,) + slot.shape, slot.dtype)
        line_all = put(line_all, slot, self.line)
        for shift in range(1, line_size):
            came = self.send(slot, line=shift)
            line_all = put(line_all, came, (self.line - shift) % line_size)
        half = line_size // 2
        from_group = self.send(line_all, group=1)
        from_pair = self.send(line_all, pair=1)
        far_low = self.send(from_group[:half], pair=1)
        far_high = self.send(from_pair[half:], group=1)
        far = jnp.concatenate([far_low, far_high], axis=0)
        pieces = []
        for group_at in range(group_size):
            for pair_at in range(pair_size):
                same_group = self.group == group_at
                same_pair = self.pair == pair_at
                pieces.append(
                    jnp.where(
                        same_group,
                        jnp.where(same_pair, line_all, from_pair),
                        jnp.where(same_pair, from_group, far),
                    )
                )
        return pieces

    def scatter_chips(self, slots):
        group_size, line_size, pair_size, _ = self.sizes
        half = line_size // 2

        def block(group_move, pair_move):
            at_group = lax.dynamic_index_in_dim(
                slots, (self.group + group_move) % group_size, 0, keepdims=False
            )
            return lax.dynamic_index_in_dim(
                at_group, (self.pair + pair_move) % pair_size, 1, keepdims=False
            )

        far = block(1, 1)
        by_group = self.send(far[:half], group=1)
        by_pair = self.send(far[half:], pair=1)
        to_pair = block(0, 1)
        to_group = block(1, 0)
        to_pair = jnp.concatenate([add_low(to_pair[:half], by_group), to_pair[half:]], axis=0)
        to_group = jnp.concatenate([to_group[:half], add_low(to_group[half:], by_pair)], axis=0)
        got_pair = self.send(to_pair, pair=1)
        got_group = self.send(to_group, group=1)
        mine = (widen(block(0, 0)) + widen(got_pair) + widen(got_group)).astype(slots.dtype)
        total = widen(lax.dynamic_index_in_dim(mine, self.line, 0, keepdims=False))
        for shift in range(1, line_size):
            out = lax.dynamic_index_in_dim(mine, (self.line + shift) % line_size, 0, keepdims=False)
            total = total + widen(self.send(out, line=shift))
        return total

    def sum_all(self, value):
        value = value + self.send(value, core=1)
        value = value + self.send(value, pair=1)
        value = value + self.send(value, group=1)
        total = value
        for shift in range(1, self.sizes[1]):
            total = total + self.send(value, line=shift)
        return total

    def by_core(self, own, other):
        return jnp.where(self.core == 0, own, other), jnp.where(self.core == 0, other, own)


def put(array, value, at):
    return lax.dynamic_update_index_in_dim(array, value, at, 0)


def widen(value):
    return value.astype(jnp.float32)


def add_low(left, right):
    return (widen(left) + widen(right)).astype(left.dtype)


def shards(
    mesh_sizes,
    block_input,
    out_cotangent,
    segment_ids,
    document_start,
    mixer_master,
    feed_master,
    mixer_first,
    feed_first,
    mixer_second,
    feed_second,
):
    local_count, sequence_length, width = block_input.shape
    row_count = local_count * sequence_length
    head_size = width // HEADS
    low = jnp.bfloat16
    wires = Wires(*device_layout(mesh_sizes))
    group_size, line_size, pair_size, _ = wires.sizes
    chips = group_size * line_size * pair_size
    core = wires.core

    mixer_shard, feed_shard = mixer_master.shape[0], feed_master.shape[0]
    feed_all = feed_shard * CORES * chips
    hidden_units = feed_all // (3 * width)
    project_width, expand_width = 3 * width, 2 * hidden_units
    project_half = project_width // 2
    lead = 8 * project_width - 2 * width
    mixer_all = mixer_shard * CORES * chips
    starts = []
    window = 0
    for chip in range(chips):
        begin = lead + chip * CORES * mixer_shard
        first_row = begin // project_width // 8 * 8
        starts.append(first_row)
        last_row = -(-(begin + CORES * mixer_shard) // project_width)
        window = max(window, last_row - first_row)
    window = -(-window // 8) * 8
    starts_array = jnp.asarray(starts, jnp.int32)
    offset = (
        lead
        + wires.chip * (CORES * mixer_shard)
        - lax.dynamic_index_in_dim(starts_array, wires.chip, 0, keepdims=False) * project_width
    )
    feed_rows = CORES * feed_shard // expand_width

    mixer_low = mixer_master.astype(low)
    feed_low = feed_master.astype(low)
    cot_rows = out_cotangent.reshape(row_count, width)
    cot_partner = wires.send(cot_rows, core=1)
    mixer_other = wires.send(mixer_low, core=1)
    feed_other = wires.send(feed_low, core=1)
    mixer_chip = jnp.concatenate(wires.by_core(mixer_low, mixer_other))
    mixer_slot = lax.dynamic_update_slice(
        jnp.zeros((window * project_width,), low), mixer_chip, (offset,)
    ).reshape(window, project_width)
    mixer_slot = jnp.where(core == 0, mixer_slot[:, :project_half], mixer_slot[:, project_half:])
    feed_chip = jnp.concatenate(wires.by_core(feed_low, feed_other)).reshape(
        feed_rows, expand_width
    )
    feed_slot = jnp.where(core == 0, feed_chip[:, :hidden_units], feed_chip[:, hidden_units:])

    mixer_pieces = wires.gather_chips(mixer_slot)
    feed_pieces = wires.gather_chips(feed_slot)

    def at_chip(pieces, chip):
        pair_at = chip % pair_size
        line_at = chip // pair_size % line_size
        return pieces[chip // (pair_size * line_size) * pair_size + pair_at][line_at]

    blocks = []
    for chip in range(chips):
        rows = at_chip(mixer_pieces, chip)
        begin = starts[chip]
        end = starts[chip + 1] if chip + 1 < chips else starts[chip] + window
        shared = max(0, starts[chip - 1] + window - begin) if chip else 0
        if shared:
            before = at_chip(mixer_pieces, chip - 1)[window - shared :]
            blocks.append(rows[:shared] + before)
        blocks.append(rows[shared : end - begin])
    mixer_half = jnp.concatenate(blocks, axis=0)
    mixer_half_other = wires.send(mixer_half, core=1)
    feed_half = jnp.concatenate(
        [at_chip(feed_pieces, chip) for chip in range(chips)], axis=0
    )
    feed_half_other = wires.send(feed_half, core=1)

    def both_halves(own, other):
        return jnp.concatenate(wires.by_core(own, other), axis=1)

    gains = both_halves(mixer_half[:8], mixer_half_other[:8]).reshape(-1)[-2 * width :]
    gain_first = gains[:width].astype(jnp.float32)
    gain_second = gains[width:].astype(jnp.float32)
    project_own = mixer_half[8 : 8 + width]
    project_other = mixer_half_other[8 : 8 + width]
    output_rows = -(-width * width // project_width)
    weight_output = (
        both_halves(
            mixer_half[8 + width : 8 + width + output_rows],
            mixer_half_other[8 + width : 8 + width + output_rows],
        )
        .reshape(-1, width)[:width]
    )
    expand_own, expand_other = feed_half[:width], feed_half_other[:width]
    weight_contract = both_halves(feed_half[width:], feed_half_other[width:]).reshape(
        hidden_units, width
    )

    first_index = (
        wires.index * local_count + jnp.arange(local_count, dtype=jnp.int32)
    ) * sequence_length
    positions = (
        first_index[:, None]
        + jnp.arange(sequence_length, dtype=jnp.int32)[None, :]
        - document_start
    )
    cosine, sine_part = rope_tables(positions, head_size)
    residual_in = block_input.reshape(row_count, width).astype(jnp.float32)
    normed_out, normed_one, spread_one = layer_norm(residual_in, gain_first)
    hidden_one = normed_out.astype(low)
    hidden_one_partner = wires.send(hidden_one, core=1)
    projected = both_halves(
        jnp.dot(hidden_one, project_own, preferred_element_type=jnp.float32),
        jnp.dot(hidden_one, project_other, preferred_element_type=jnp.float32),
    ).reshape(local_count, sequence_length, 3, HEADS, head_size)
    query_rope = rotate_pairs(projected[:, :, 0], cosine, sine_part).astype(low)
    key_rope = rotate_pairs(projected[:, :, 1], cosine, sine_part).astype(low)
    value_rows = projected[:, :, 2].astype(low)
    context_heads, log_total = lax.map(
        attend_forward, (query_rope, key_rope, value_rows, segment_ids)
    )
    context = context_heads.reshape(row_count, width)
    context_partner = wires.send(context, core=1)
    residual_mid = residual_in + jnp.dot(context, weight_output, preferred_element_type=jnp.float32)
    normed_out, normed_two, spread_two = layer_norm(residual_mid, gain_second)
    hidden_two = normed_out.astype(low)
    hidden_two_partner = wires.send(hidden_two, core=1)
    gelu_input, gate_part = wires.by_core(
        jnp.dot(hidden_two, expand_own, preferred_element_type=jnp.float32),
        jnp.dot(hidden_two, expand_other, preferred_element_type=jnp.float32),
    )
    activated, gelu_slope = gelu_parts(gelu_input)
    product = (activated * gate_part).astype(low)
    product_partner = wires.send(product, core=1)
    block_output = (
        residual_mid + jnp.dot(product, weight_contract, preferred_element_type=jnp.float32)
    ).astype(low)

    def two_rows(own, partner):
        return jnp.concatenate([own, partner], axis=0)

    def weight_gradient(inputs, inputs_partner, back, back_partner):
        return lax.dot_general(
            two_rows(inputs, inputs_partner),
            two_rows(back, back_partner),
            (((0,), (0,)), ((), ())),
            preferred_element_type=jnp.float32,
        ).astype(low)

    cotangent = cot_rows
    back_contract = weight_gradient(product, product_partner, cotangent, cot_partner)
    back_product = jnp.dot(cotangent, weight_contract.T, preferred_element_type=jnp.float32)
    back_gelu = (back_product * gate_part * gelu_slope).astype(low)
    back_gate = (back_product * activated).astype(low)
    back_own, back_send = wires.by_core(back_gelu, back_gate)
    back_came = wires.send(back_send, core=1)
    back_expand = weight_gradient(hidden_two, hidden_two_partner, back_own, back_came)
    back_hidden = lax.dot_general(
        back_own, expand_own, (((1,), (1,)), ((), ())), preferred_element_type=jnp.float32
    ) + lax.dot_general(
        back_send, expand_other, (((1,), (1,)), ((), ())), preferred_element_type=jnp.float32
    )
    contract_rows = back_contract.reshape(-1, expand_width)
    contract_half = jnp.where(
        core == 0, contract_rows[:, :hidden_units], contract_rows[:, hidden_units:]
    )
    feed_slots = jnp.concatenate([back_expand, contract_half], axis=0).reshape(
        group_size, line_size, pair_size, feed_rows, hidden_units
    )
    feed_sum = wires.scatter_chips(feed_slots)

    back_norm, back_gain_two = norm_backward(back_hidden, normed_two, spread_two, gain_second)
    back_mid = cotangent.astype(jnp.float32) + back_norm
    back_mid_low = back_mid.astype(low)
    back_mid_partner = wires.send(back_mid_low, core=1)
    back_output = weight_gradient(context, context_partner, back_mid_low, back_mid_partner)
    back_context = (
        lax.dot_general(
            back_mid_low,
            weight_output,
            (((1,), (1,)), ((), ())),
            preferred_element_type=jnp.float32,
        )
        .astype(low)
        .reshape(local_count, sequence_length, HEADS, head_size)
    )
    back_query, back_key, back_values = lax.map(
        attend_backward,
        (query_rope, key_rope, value_rows, segment_ids, log_total, back_context, context_heads),
    )
    back_query = rotate_pairs(back_query, cosine, -sine_part)
    back_key = rotate_pairs(back_key, cosine, -sine_part)
    back_projected = (
        jnp.stack([back_query, back_key, back_values], axis=2)
        .reshape(row_count, 3 * width)
        .astype(low)
    )
    low_half, high_half = back_projected[:, :project_half], back_projected[:, project_half:]
    back_own, back_send = wires.by_core(low_half, high_half)
    back_came = wires.send(back_send, core=1)
    back_project = weight_gradient(hidden_one, hidden_one_partner, back_own, back_came)
    back_hidden = lax.dot_general(
        back_own, project_own, (((1,), (1,)), ((), ())), preferred_element_type=jnp.float32
    ) + lax.dot_general(
        back_send, project_other, (((1,), (1,)), ((), ())), preferred_element_type=jnp.float32
    )
    back_norm, back_gain_one = norm_backward(back_hidden, normed_one, spread_one, gain_first)
    input_gradient = back_mid + back_norm

    back_gains = jnp.concatenate([back_gain_one, back_gain_two])
    back_gains = (back_gains + wires.send(back_gains, core=1)).astype(low)
    gain_rows = jnp.concatenate([jnp.zeros((lead,), low), back_gains]).reshape(8, project_width)
    gain_half = jnp.where(core == 0, gain_rows[:, :project_half], gain_rows[:, project_half:])
    total_rows = starts[-1] + window
    output_pad = (total_rows - 8 - width) * project_width - width * width
    output_flat = jnp.concatenate([back_output.reshape(-1), jnp.zeros((output_pad,), low)])
    output_flat = output_flat.reshape(-1, project_width)
    output_half = jnp.where(
        core == 0, output_flat[:, :project_half], output_flat[:, project_half:]
    )
    mixer_rows = jnp.concatenate([gain_half, back_project, output_half], axis=0)
    mixer_slots = jnp.stack([mixer_rows[at : at + window] for at in starts]).reshape(
        group_size, line_size, pair_size, window, project_half
    )
    mixer_sum = wires.scatter_chips(mixer_slots)

    feed_rows_own = feed_rows // CORES
    feed_out = lax.dynamic_slice_in_dim(feed_sum, (1 - core) * feed_rows_own, feed_rows_own, 0)
    feed_mine = lax.dynamic_slice_in_dim(feed_sum, core * feed_rows_own, feed_rows_own, 0)
    feed_gradient = both_halves(feed_mine, wires.send(feed_out, core=1)).reshape(-1)
    mixer_whole = both_halves(mixer_sum, wires.send(mixer_sum, core=1)).reshape(-1)
    mixer_gradient = lax.dynamic_slice(
        mixer_whole, (offset + core * mixer_shard,), (mixer_shard,)
    )

    square_total = wires.sum_all(
        jnp.sum(mixer_gradient * mixer_gradient) + jnp.sum(feed_gradient * feed_gradient)
    )
    clip_factor = jnp.minimum(1.0, clip_norm / (jnp.sqrt(square_total) + 1e-06))
    mixer_new, mixer_first_new, mixer_second_new = optimizer_step(
        mixer_master, mixer_first, mixer_second, mixer_gradient, clip_factor
    )
    feed_new, feed_first_new, feed_second_new = optimizer_step(
        feed_master, feed_first, feed_second, feed_gradient, clip_factor
    )
    return (
        block_output.reshape(local_count, sequence_length, width),
        input_gradient.reshape(local_count, sequence_length, width),
        mixer_gradient,
        feed_gradient,
        mixer_new,
        feed_new,
        mixer_first_new,
        feed_first_new,
        mixer_second_new,
        feed_second_new,
    )


def solution(mesh):
    sizes = (mesh.shape["group"], mesh.shape["wide"])
    return jax.shard_map(
        functools.partial(shards, sizes),
        mesh=mesh,
        in_specs=(
            P(("group", "wide"), None, None),
            P(("group", "wide"), None, None),
            P(("group", "wide"), None),
            P(("group", "wide"), None),
            P(("group", "wide")),
            P(("group", "wide")),
            P(("group", "wide")),
            P(("group", "wide")),
            P(("group", "wide")),
            P(("group", "wide")),
        ),
        out_specs=(
            P(("group", "wide"), None, None),
            P(("group", "wide"), None, None),
            P(("group", "wide")),
            P(("group", "wide")),
            P(("group", "wide")),
            P(("group", "wide")),
            P(("group", "wide")),
            P(("group", "wide")),
            P(("group", "wide")),
            P(("group", "wide")),
        ),
        check_vma=False,
    )
```
